32 devices in a mesh: dp: 4 (over y, core), head: 8 (over z, x).
Axes of the slice: x: 2, y: 2, z: 4, core: 2. Of those that a mesh axis runs over, the one named last changes fastest.
Arguments:
- hidden: bfloat16 [12288, 4096], P('dp'), may hold values from -6 to 6
- weight: bfloat16 [2048, 4096], P('head'), may hold values from -0.09375 to 0.09375
- block_ids: int32 [48, 8], P('dp'), may hold values from 0 to 15, all different within a row
- targets: int32 [12288, 8], P('dp'), may hold values from 0 to 2047
Outputs:
- grad_hidden: bfloat16 [12288, 4096], P('dp', 'head')
- grad_weight: bfloat16 [2048, 4096], P('head', 'dp')
The draws below stay inside these ranges and needn't reach their ends.
Inputs may be any that keep to these rules, and one draw needn't show every extreme that they name: `block_ids`: each row block lists 8 different label blocks; every label block is listed by some row block. `targets`: a row may repeat a label id.
All inputs are finite; a program needn't handle non-finite values.
Results may differ from the reference program's by a relative error of at most 0.014.
Values may be sent and summed in bfloat16 or wider, within the bound.
No kernel may reach another device: no remote copies, remote signals or barrier semaphores. Data moves between devices by JAX's collectives and lax.ppermute only.
A program may use at most 192 MiB of HBM per device.

```python
import jax
import jax.numpy as jnp
from jax import lax

D = 4096
BLOCK = 128
ROWBLK = 256
SLOTS = 8
POS = 8
BPD = 2
NB = 16
LABELS = 2048
RBT = 48
ROWS = 12288
N_HEAD = 8


def touch_ends(values, rng, low, largest):
    longest = values.shape.index(max(values.shape))
    spots = []
    for shift in (0, 1):
        where = [jax.random.randint(jax.random.fold_in(rng, axis), (), 0, length) for axis, length in enumerate(values.shape)]
        where[longest] = (where[longest] + shift) % values.shape[longest]
        spots.append(tuple(where))
    return values.at[spots[0]].set(low).at[spots[1]].set(largest)


def block_scale(key, dims, shards, smallest, high):
    def one(dim, shards_of):
        draws = jax.random.uniform(jax.random.fold_in(jax.random.fold_in(key, 6), dim), (shards_of,), jnp.float32, smallest / len(shards), high / len(shards))
        return jnp.repeat(jnp.exp(draws), dims[dim] // shards_of).reshape((-1,) + (1,) * (len(dims) - dim - 1))

    factor_of = one(*shards[0])
    for cut in shards[1:]:
        factor_of = factor_of * one(*cut)
    return factor_of


def choose_distinct(own_key, rows, count, top, lift):
    ranking = jax.random.permutation(jax.random.fold_in(own_key, 1), count)
    favour = ranking
    for power in range(3):
        favour = favour * favour // count
    favour = favour * lift // count
    lots = jax.random.randint(jax.random.fold_in(own_key, 2), (rows, count), 0, 4096) + favour
    holders = jax.random.permutation(jax.random.fold_in(own_key, 3), rows)[jnp.arange(count) % rows]
    lots = jnp.where(jnp.arange(rows)[:, None] == holders[None, :], 1 << 14, lots)
    score = lots * count + jnp.arange(count)
    return lax.top_k(score.astype(jnp.int32), top)[1].astype(jnp.int32)


def bell_draw(key, shape, scale, most, cuts=(), held_as=jnp.bfloat16):
    level = block_scale(key, shape, cuts, -0.22, 0.18) if cuts else 1.0
    drawn = jax.random.normal(key, shape, jnp.float32) * scale * level
    return jnp.minimum(jnp.maximum(drawn, -most), most).astype(held_as)


def setup_inputs(seed: int = 0) -> dict:
    streams_of = jax.random.split(jax.random.key(seed), 5)
    return {
        "hidden": bell_draw(streams_of[0], (ROWS, D), 1.0, 6.0, ((0, 4),)),
        "weight": bell_draw(streams_of[1], (LABELS, D), D ** -0.5, 0.09375, ((0, 8),)),
        "block_ids": choose_distinct(streams_of[2], RBT, NB, SLOTS, 8192),
        "targets": touch_ends(jax.random.randint(streams_of[3], (ROWS, POS), 0, LABELS), jax.random.fold_in(streams_of[3], 1), 0, LABELS - 1).astype(jnp.int32),
    }


def reference(hidden, weight, block_ids, targets):
    blocks = weight.reshape(NB, BLOCK, D)
    hid3 = hidden.reshape(RBT, ROWBLK, D)
    tgt3 = targets.reshape(RBT, ROWBLK, POS)
    offsets = jnp.arange(BLOCK, dtype=jnp.int32)
    groups = jnp.arange(N_HEAD, dtype=jnp.int32)

    def step(carry, item):
        rows, ids, tgt = item
        chosen = blocks[ids]
        logits = jnp.dot(rows, chosen.reshape(SLOTS * BLOCK, D).T, preferred_element_type=jnp.float32)
        labels = (ids[:, None] * BLOCK + offsets[None, :]).reshape(-1)
        hits = jnp.any(tgt[:, :, None] == labels[None, None, :], axis=1)
        grads = (jax.nn.sigmoid(logits) - hits.astype(jnp.float32)).astype(jnp.bfloat16)
        grads3 = grads.reshape(ROWBLK, SLOTS, BLOCK).astype(jnp.float32)
        terms = jnp.einsum('rkj,kjd->krd', grads3, chosen.astype(jnp.float32))
        owner = ((ids // BPD)[:, None] == groups[None, :]).astype(jnp.float32)
        parts = jnp.einsum('ko,krd->ord', owner, terms, precision=lax.Precision.HIGHEST)
        rounded = lax.optimization_barrier(parts.astype(jnp.bfloat16))
        grad_rows = jnp.sum(rounded.astype(jnp.float32), axis=0).astype(jnp.bfloat16)
        contrib = jnp.einsum('rkj,rd->kjd', grads3, rows.astype(jnp.float32))
        carry = carry.at[ids].add(contrib)
        return carry, grad_rows

    start = jnp.zeros((NB, BLOCK, D), jnp.float32)
    total, grad_rows = lax.scan(step, start, (hid3, block_ids, tgt3))
    grad_hidden = grad_rows.reshape(ROWS, D)
    grad_weight = total.reshape(LABELS, D).astype(jnp.bfloat16)
    return grad_hidden, grad_weight
```

```python
import functools

import jax
import jax.numpy as jnp
import numpy as np
from jax import lax
from jax.experimental import pallas as pl
from jax.experimental.pallas import tpu as pltpu
from jax.sharding import PartitionSpec as P


BLOCK = 128
PAIR = 2 * BLOCK
Z = 4


def ring_order(heads):
    order = []
    for x in range(heads // Z):
        zs = range(Z) if x % 2 == 0 else reversed(range(Z))
        order += [z * (heads // Z) + x for z in zs]
    return order


def signal_of(logits, targets, labels):
    hit = targets[:, 0:1] == labels
    for p in range(1, targets.shape[1]):
        hit = jnp.logical_or(hit, targets[:, p : p + 1] == labels)
    prob = 0.5 * jnp.tanh(0.5 * logits) + 0.5
    return prob - hit.astype(jnp.float32)


def listed_flag(ids_ref, i, block):
    flag = ids_ref[0, i] == block
    for k in range(1, ids_ref.shape[0]):
        flag = jnp.logical_or(flag, ids_ref[k, i] == block)
    return flag.astype(jnp.int32)


def lanes():
    return lax.broadcasted_iota(jnp.int32, (1, PAIR), 1)


def nt(a, b):
    return lax.dot_general(a, b, (((1,), (1,)), ((), ())), preferred_element_type=jnp.float32)


def tn(a, b):
    return lax.dot_general(a, b, (((0,), (0,)), ((), ())), preferred_element_type=jnp.float32)


def rows_of(i, tile):
    return pl.ds(pl.multiple_of(i * tile, tile), tile)


def pipelined(count, first_half, second_half, log_ref):
    @pl.when(count > 0)
    def _():
        log_ref[...] = first_half(0)

        def body(n, carry):
            ready = log_ref[...]
            following = first_half(n)
            second_half(n - 1, ready)
            log_ref[...] = following
            return carry

        lax.fori_loop(1, count, body, 0)
        second_half(count - 1, log_ref[...])


def own_kernel(
    meta, ids, src_ref, t_ref, w_ref, h_ref, acc_ref, keep_ref, send_ref, gw_ref, log_ref, task_ref, sem, *, parts
):
    row_blocks = ids.shape[1]
    tile = h_ref.shape[0] // row_blocks
    narrow = acc_ref.shape[1]
    b0 = meta[0] * 2

    def load(i):
        rows = rows_of(i, tile)
        return pltpu.make_async_copy(src_ref.at[rows, :], h_ref.at[rows, :], sem.at[i])

    def start_load(i, carry):
        load(i).start()
        return carry

    def wait_load(i, carry):
        load(i).wait()
        return carry

    lax.fori_loop(0, row_blocks, start_load, 0)
    acc_ref[...] = jnp.zeros_like(acc_ref)
    gw_ref[...] = jnp.zeros_like(gw_ref)

    def list_tasks(i, count):
        m0 = listed_flag(ids, i, b0)
        m1 = listed_flag(ids, i, b0 + 1)

        @pl.when(m0 + m1 > 0)
        def _():
            task_ref[0, count] = i
            task_ref[1, count] = m0
            task_ref[2, count] = m1

        return count + jnp.maximum(m0, m1)

    count = lax.fori_loop(0, row_blocks, list_tasks, jnp.int32(0))
    cols = pl.ds(pl.multiple_of(meta[0] * narrow, 128), narrow)

    def first_half(n):
        i = task_ref[0, n]
        past = -1 if isinstance(n, int) else task_ref[0, n - 1]
        lax.fori_loop(past + 1, i + 1, wait_load, 0)
        return nt(h_ref[rows_of(i, tile), :], w_ref[...])

    def second_half(n, logits):
        i = task_ref[0, n]
        rows = rows_of(i, tile)
        keep = jnp.where(lanes() < BLOCK, task_ref[1, n], task_ref[2, n]) > 0
        signal = signal_of(logits, t_ref[:, rows].T, b0 * BLOCK + lanes())
        g = jnp.where(keep, signal, 0.0).astype(jnp.bfloat16)
        acc_ref[rows, :] = jnp.dot(g, w_ref[:, cols], preferred_element_type=jnp.float32)
        gw_ref[...] += tn(g, h_ref[rows, :])

    pipelined(count, first_half, second_half, log_ref)
    done = jnp.where(count > 0, task_ref[0, jnp.maximum(count - 1, 0)], -1)
    lax.fori_loop(done + 1, row_blocks, wait_load, 0)
    core = meta[1]
    wide = keep_ref.shape[2]
    for y in range(parts // 2):
        mine = pl.ds(pl.multiple_of((2 * y + core) * wide, 128), wide)
        other = pl.ds(pl.multiple_of((2 * y + 1 - core) * wide, 128), wide)
        keep_ref[y] = gw_ref[:, mine]
        send_ref[y] = gw_ref[:, other].astype(jnp.bfloat16)


VM = pltpu.VMEM
SCALARS = [pl.BlockSpec(memory_space=pltpu.SMEM)] * 2


def in_vmem(n):
    return [pl.BlockSpec(memory_space=VM)] * n


def own_stage(meta, ids, hidden, targets, weight, narrow, parts):
    rows, d = hidden.shape
    owned = weight.shape[0]
    wide = d // parts
    row_blocks = ids.shape[1]
    return pl.pallas_call(
        functools.partial(own_kernel, parts=parts),
        in_specs=SCALARS + [pl.BlockSpec(memory_space=pl.ANY)] + in_vmem(2),
        out_specs=in_vmem(4),
        out_shape=[
            VM((rows, d), hidden.dtype),
            VM((rows, narrow), jnp.float32),
            jax.ShapeDtypeStruct((parts // 2, owned, wide), jnp.float32),
            jax.ShapeDtypeStruct((parts // 2, owned, wide), jnp.bfloat16),
        ],
        scratch_shapes=[
            VM((owned, d), jnp.float32),
            VM((rows // row_blocks, PAIR), jnp.float32),
            pltpu.SMEM((3, row_blocks), jnp.int32),
            pltpu.SemaphoreType.DMA((row_blocks,)),
        ],
        cost_estimate=pl.CostEstimate(flops=4 * rows * owned * d, bytes_accessed=1 << 22, transcendentals=0),
        compiler_params=pltpu.CompilerParams(vmem_limit_bytes=20 << 20),
        name="own_stage",
    )(meta, ids, hidden, targets, weight)


def far_kernel(meta, ids, h_ref, t_ref, acc_ref, *rest, shards, places):
    pieces = rest[: len(places)]
    *_, out_ref, w_ref, log_ref, task_ref, sem = rest[len(places) :]
    row_blocks = ids.shape[1]
    tile = h_ref.shape[0] // row_blocks
    narrow = acc_ref.shape[1]
    copies = [
        pltpu.make_async_copy(piece, w_ref.at[j, :, pl.ds(col, piece.shape[1])], sem.at[k])
        for k, (piece, (j, col)) in enumerate(zip(pieces, places))
    ]
    for copy in copies:
        copy.start()
    core = meta[1]
    names = []
    for s in shards:
        names += [meta[s] * 2 + core, meta[s] * 2 + 1 - core]

    def list_tasks(i, count):
        for j in range(0, len(names)):
            flag = listed_flag(ids, i, names[j])

            @pl.when(flag > 0)
            def _(j=j, count=count):
                fresh = count % 2
                task_ref[fresh, count // 2] = j
                task_ref[2 + fresh, count // 2] = names[j]
                task_ref[4, count // 2] = i
                task_ref[5, count // 2] = (1 + fresh) * BLOCK

            count = count + flag
        odd = count % 2

        @pl.when(odd > 0)
        def _():
            task_ref[1, count // 2] = 0
            task_ref[3, count // 2] = 0

        return count + odd

    count = lax.fori_loop(0, row_blocks, list_tasks, jnp.int32(0)) // 2
    cols = pl.ds(pl.multiple_of(meta[0] * narrow, 128), narrow)
    for copy in copies:
        copy.wait()

    def first_half(n):
        both = jnp.concatenate([w_ref[task_ref[0, n]], w_ref[task_ref[1, n]]], axis=0)
        return nt(h_ref[rows_of(task_ref[4, n], tile), :], both)

    def second_half(n, logits):
        rows = rows_of(task_ref[4, n], tile)
        lane = lanes()
        labels = jnp.where(lane < BLOCK, task_ref[2, n] * BLOCK + lane, (task_ref[3, n] - 1) * BLOCK + lane)
        signal = signal_of(logits, t_ref[:, rows].T, labels)
        g = jnp.where(lane < task_ref[5, n], signal, 0.0).astype(jnp.bfloat16)
        thin = jnp.concatenate([w_ref[task_ref[0, n], :, cols], w_ref[task_ref[1, n], :, cols]], axis=0)
        acc_ref[rows, :] += jnp.dot(g, thin, preferred_element_type=jnp.float32)

    pipelined(count, first_half, second_half, log_ref)
    if out_ref.dtype != jnp.float32:
        out_ref[...] = acc_ref[...].astype(out_ref.dtype)


def far_stage(meta, ids, hidden, targets, acc, pieces, places, shards, last):
    rows, d = hidden.shape
    narrow = acc.shape[1]
    row_blocks = ids.shape[1]
    blocks = 2 * len(shards)
    if last:
        shape = [jax.ShapeDtypeStruct((rows, narrow), jnp.bfloat16)]
    else:
        shape = [VM((rows, d), hidden.dtype), VM((rows, narrow), jnp.float32)]
    return pl.pallas_call(
        functools.partial(far_kernel, shards=shards, places=places),
        in_specs=SCALARS + in_vmem(3) + [pl.BlockSpec(memory_space=pl.ANY)] * len(pieces),
        out_specs=in_vmem(len(shape)),
        out_shape=shape,
        scratch_shapes=[
            VM((blocks, BLOCK, d), jnp.bfloat16),
            VM((rows // row_blocks, PAIR), jnp.float32),
            pltpu.SMEM((6, row_blocks * len(shards)), jnp.int32),
            pltpu.SemaphoreType.DMA((len(pieces),)),
        ],
        input_output_aliases={} if last else {2: 0, 4: 1},
        cost_estimate=pl.CostEstimate(flops=2 * rows * blocks * BLOCK * d, bytes_accessed=1 << 22, transcendentals=0),
        compiler_params=pltpu.CompilerParams(vmem_limit_bytes=20 << 20),
        name="far_stage",
    )(meta, ids, hidden, targets, acc, *pieces)


def merge_kernel(part, keep_ref, near_ref, mine_ref, *away_refs):
    row = part[0] // 2
    count = keep_ref.shape[0]
    mine_ref[...] = keep_ref[row] + near_ref[row].astype(jnp.float32)
    for k, away_ref in enumerate(away_refs):
        ahead = (row + k + 1) % count
        away_ref[...] = (keep_ref[ahead] + near_ref[ahead].astype(jnp.float32)).astype(away_ref.dtype)


def merge(part, keep, near):
    count, owned, wide = keep.shape
    outs = [jax.ShapeDtypeStruct((owned, wide), jnp.float32)]
    outs += [jax.ShapeDtypeStruct((owned, wide), jnp.bfloat16)] * (count - 1)
    return pl.pallas_call(
        merge_kernel,
        in_specs=SCALARS[:1] + in_vmem(2),
        out_specs=in_vmem(count),
        out_shape=outs,
        compiler_params=pltpu.CompilerParams(vmem_limit_bytes=8 << 20),
        name="merge",
    )(part.reshape(1), keep, near)


def finish_kernel(mine_ref, *refs):
    total = mine_ref[...]
    for got in refs[:-1]:
        total = total + got[...].astype(jnp.float32)
    refs[-1][...] = total.astype(refs[-1].dtype)


def finish(mine, got):
    return pl.pallas_call(
        finish_kernel,
        in_specs=in_vmem(1 + len(got)),
        out_specs=pl.BlockSpec(memory_space=VM),
        out_shape=jax.ShapeDtypeStruct(mine.shape, jnp.bfloat16),
        compiler_params=pltpu.CompilerParams(vmem_limit_bytes=8 << 20),
        name="finish",
    )(mine, *got)


def halves_kernel(a_ref, b_ref, low_ref, high_ref, sem):
    half = low_ref.shape[1]
    low = pltpu.make_async_copy(a_ref.at[:, :half], low_ref, sem.at[0])
    high = pltpu.make_async_copy(b_ref.at[:, half:], high_ref, sem.at[1])
    low.start()
    high.start()
    low.wait()
    high.wait()


def halves(a, b):
    whole = pl.BlockSpec(memory_space=pl.ANY)
    return pl.pallas_call(
        halves_kernel,
        in_specs=[whole] * 2,
        out_specs=[whole] * 2,
        out_shape=[jax.ShapeDtypeStruct((a.shape[0], a.shape[1] // 2), a.dtype)] * 2,
        scratch_shapes=[pltpu.SemaphoreType.DMA((2,))],
        compiler_params=pltpu.CompilerParams(vmem_limit_bytes=1 << 20),
        name="halves",
    )(a, b)


def local(hidden, weight, block_ids, targets):
    heads = lax.axis_size("head")
    parts = lax.axis_size("dp")
    head = lax.axis_index("head")
    part = lax.axis_index("dp")
    core = part % 2
    d = hidden.shape[1]
    narrow = d // heads
    half = heads // 2
    order = ring_order(heads)
    spot = np.argsort(order)
    table = np.zeros((heads, heads + 1), np.int32)
    for k in range(heads):
        table[k, 0] = k
        for step in range(1, half):
            table[k, 2 * step] = order[(spot[k] - step) % heads]
            table[k, 2 * step + 1] = order[(spot[k] + step) % heads]
        table[k, heads] = order[(spot[k] + half) % heads]
    column = np.arange(heads + 1) == 1
    meta = jnp.where(column, core, jnp.asarray(table)[head]).astype(jnp.int32)
    forward = [(order[k], order[(k + 1) % heads]) for k in range(heads)]
    backward = [(b, a) for a, b in forward]
    cores = [(p, p ^ 1) for p in range(parts)]
    ids = block_ids.T
    marks = pltpu.with_memory_space_constraint(targets.T, VM)

    own = lax.dynamic_slice_in_dim(weight, core * BLOCK, BLOCK, axis=0)
    fwd = lax.ppermute(own, "head", forward)
    bwd = lax.ppermute(own, "head", backward)

    rows, acc, keep, away = own_stage(meta, ids, hidden, marks, weight, narrow, parts)

    near = lax.ppermute(away, "dp", cores)
    mine, *away = merge(part, keep, near)
    got = [
        lax.ppermute(away[k - 1], "dp", [(p, (p + 2 * k) % parts) for p in range(parts)])
        for k in range(1, parts // 2)
    ]
    grad_weight = finish(mine, got)

    for step in range(1, half):
        fwd_swap = lax.ppermute(fwd, "dp", cores)
        bwd_swap = lax.ppermute(bwd, "dp", cores)
        pieces = [fwd, fwd_swap, bwd, bwd_swap]
        places = [(0, 0), (1, 0), (2, 0), (3, 0)]
        if step + 1 == half:
            fwd, bwd = halves(fwd, bwd)
        fwd = lax.ppermute(fwd, "head", forward)
        bwd = lax.ppermute(bwd, "head", backward)
        rows, acc = far_stage(
            meta, ids, rows, marks, acc, pieces, places, [2 * step, 2 * step + 1], False
        )

    fwd_swap = lax.ppermute(fwd, "dp", cores)
    bwd_swap = lax.ppermute(bwd, "dp", cores)
    pieces = [fwd, bwd, fwd_swap, bwd_swap]
    places = [(0, 0), (0, d // 2), (1, 0), (1, d // 2)]
    (grad_hidden,) = far_stage(meta, ids, rows, marks, acc, pieces, places, [heads], True)
    return (grad_hidden, grad_weight)


def solution(mesh):
    return jax.shard_map(
        local,
        mesh=mesh,
        in_specs=(P("dp", None), P("head", None), P("dp", None), P("dp", None)),
        out_specs=(P("dp", "head"), P("head", "dp")),
        check_vma=False,
    )
```
